512 devices in a mesh: dp: 8 (over y), ctx: 64 (over z, x, core).
Axes of the slice: x: 4, y: 8, z: 8, core: 2. Of those that a mesh axis runs over, the one named last changes fastest.
Arguments:
- queries: bfloat16 [8, 8192, 1024], P('dp', 'ctx'), may hold values from -6 to 6
- keys: bfloat16 [8, 8192, 1024], P('dp', 'ctx'), may hold values from -0.5390625 to 0.5390625
- values: bfloat16 [8, 8192, 1024], P('dp', 'ctx'), may hold values from -6 to 6
- gain: float32 [1024], replicated, may hold values from 0.1 to 1.9
- grad_out: bfloat16 [8, 8192, 1024], P('dp', 'ctx'), may hold values from -16 to 16
Outputs:
- output: bfloat16 [8, 8192, 1024], P('dp', 'ctx')
- grad_queries: bfloat16 [8, 8192, 1024], P('dp', 'ctx')
- grad_keys: bfloat16 [8, 8192, 1024], P('dp', 'ctx')
- grad_values: bfloat16 [8, 8192, 1024], P('dp', 'ctx')
- grad_gain: float32 [1024], replicated
The draws below stay inside these ranges and needn't reach their ends.
All inputs are finite; a program needn't handle non-finite values.
Results may differ from the reference program's by a relative error of at most 0.006.
Values sent between devices are 32-bit elements; how exact they have to be, the bound alone decides.
No kernel may reach another device: no remote copies, remote signals or barrier semaphores. Data moves between devices by JAX's collectives and lax.ppermute only.
A program may use at most 128 MiB of HBM per device.

```python
import jax
import jax.numpy as jnp
from jax import lax

HEADS = 16
HEAD_DIM = 64
GROUP = 128
WIDTH = 1024
SEQS = 8
LENGTH = 8192


def draw_grad_out(key, part):
    position = jnp.arange(LENGTH, dtype=jnp.float32) / (LENGTH - 1)
    base = jax.random.truncated_normal(key, -4.0, 4.0, (SEQS, LENGTH, WIDTH), jnp.float32)
    factor = 1.0 + 2.0 * position
    return (base * factor[None, :, None]).astype(jnp.bfloat16)


def levels(own_key, dims, shards, low, largest):
    level = 1.0
    for dim, blocks in shards:
        draws = jax.random.uniform(jax.random.fold_in(jax.random.fold_in(own_key, 6), dim), (blocks,), jnp.float32, low / len(shards), largest / len(shards))
        level = level * jnp.repeat(jnp.exp(draws), dims[dim] // blocks).reshape((-1,) + (1,) * (len(dims) - 1 - dim))
    return level


def noise(key, extent, deviation, bound, split=(), kind=jnp.bfloat16):
    factor_of = levels(key, extent, split, -0.22, 0.18) if split else 1.0
    entries = jax.random.normal(key, extent, jnp.float32) * deviation * factor_of
    return jnp.minimum(jnp.maximum(entries, -bound), bound).astype(kind)


def setup_inputs(seed: int = 0) -> dict:
    splits = jax.random.split(jax.random.key(seed), 6)
    return {
        "queries": noise(splits[0], (SEQS, LENGTH, WIDTH), 1.0, 6.0, ((0, 8), (1, 64))),
        "keys": noise(splits[1], (SEQS, LENGTH, WIDTH), 0.09, 0.5390625, ((0, 8), (1, 64))),
        "values": noise(splits[2], (SEQS, LENGTH, WIDTH), 1.0, 6.0, ((0, 8), (1, 64))),
        "gain": jnp.clip(1.0 + 0.18 * jax.random.normal(splits[3], (WIDTH,), jnp.float32), 0.1, 1.9),
        "grad_out": draw_grad_out(jax.random.fold_in(splits[5], 71), 0),
    }


def one_sequence(args, gain):
    queries, keys, values, grad_out = args
    blocks = LENGTH // GROUP
    shape4 = (blocks, GROUP, HEADS, HEAD_DIM)
    query_f = queries.reshape(shape4).astype(jnp.float32)
    key_f = keys.reshape(shape4).astype(jnp.float32)
    value_f = values.reshape(shape4).astype(jnp.float32)
    key_value = jnp.einsum('nrhd,nrhe->nhde', key_f, value_f)
    zeros = jnp.zeros((1, HEADS, HEAD_DIM, HEAD_DIM), jnp.float32)
    state = jnp.concatenate([zeros, jnp.cumsum(key_value, 0)[:-1]], 0)
    state_low = state.astype(jnp.bfloat16).astype(jnp.float32)
    causal = jnp.tril(jnp.ones((GROUP, GROUP), bool))
    scores = jnp.where(causal, jnp.einsum('nthd,nshd->nhts', query_f, key_f), 0.0).astype(jnp.bfloat16).astype(jnp.float32)
    attn = jnp.einsum('nhts,nshe->nthe', scores, value_f) + jnp.einsum('nthd,nhde->nthe', query_f, state_low)
    attn = attn.reshape(LENGTH, WIDTH)
    inverse_rms = lax.rsqrt(lax.optimization_barrier(jnp.mean(attn * attn, -1, keepdims=True)) + 1e-06)
    normed = attn * inverse_rms
    output = (normed * gain).astype(jnp.bfloat16)
    grad_f = grad_out.astype(jnp.float32)
    gain_part = lax.optimization_barrier(jnp.sum(grad_f * normed, 0))
    grad_norm = grad_f * gain
    grad_attn = (inverse_rms * (grad_norm - normed * lax.optimization_barrier(jnp.mean(grad_norm * normed, -1, keepdims=True)))).astype(jnp.bfloat16)
    grad_attn = grad_attn.reshape(shape4).astype(jnp.float32)
    query_grad = jnp.einsum('nthd,nthe->nhde', query_f, grad_attn)
    from_end = jnp.cumsum(query_grad[::-1], 0)[::-1]
    later = jnp.concatenate([from_end[1:], zeros], 0)
    later_low = later.astype(jnp.bfloat16).astype(jnp.float32)
    dscores = jnp.where(causal, jnp.einsum('nthe,nshe->nhts', grad_attn, value_f), 0.0).astype(jnp.bfloat16).astype(jnp.float32)
    grad_queries = jnp.einsum('nhts,nshd->nthd', dscores, key_f) + jnp.einsum('nthe,nhde->nthd', grad_attn, state_low)
    grad_keys = jnp.einsum('nhts,nthd->nshd', dscores, query_f) + jnp.einsum('nshe,nhde->nshd', value_f, later_low)
    grad_values = jnp.einsum('nhts,nthe->nshe', scores, grad_attn) + jnp.einsum('nshd,nhde->nshe', key_f, later_low)
    flat = (LENGTH, WIDTH)
    return (output, grad_queries.reshape(flat).astype(jnp.bfloat16), grad_keys.reshape(flat).astype(jnp.bfloat16), grad_values.reshape(flat).astype(jnp.bfloat16), gain_part)

def reference(queries, keys, values, gain, grad_out):
    results = lax.map(lambda a: one_sequence(a, gain), (queries, keys, values, grad_out))
    return (results[0], results[1], results[2], results[3], lax.optimization_barrier(jnp.sum(results[4], 0)))
```

```python
import jax
import jax.numpy as jnp
from jax import lax
from jax.experimental import pallas as pl
from jax.experimental.pallas import tpu as pltpu
from jax.sharding import PartitionSpec as P

HEAD_DIM = 64
PAIR = 2 * HEAD_DIM
F32 = jnp.float32
BF16 = jnp.bfloat16
VMEM = pl.BlockSpec(memory_space=pltpu.VMEM)


def mm(a, b):
    return lax.dot_general(a, b, (((1,), (0,)), ((), ())), preferred_element_type=F32)


def mm_bt(a, b):
    return lax.dot_general(a, b, (((1,), (1,)), ((), ())), preferred_element_type=F32)


def mm_at(a, b):
    return lax.dot_general(a, b, (((0,), (0,)), ((), ())), preferred_element_type=F32)


def halves():
    lane = lax.broadcasted_iota(jnp.int32, (1, PAIR), 1)
    first = jnp.where(lane < HEAD_DIM, 1.0, 0.0).astype(BF16)
    second = jnp.where(lane < HEAD_DIM, 0.0, 1.0).astype(BF16)
    return first, second


def stack(x, masks):
    return jnp.concatenate([x * masks[0], x * masks[1]], axis=0)


def pack(full):
    lane = lax.broadcasted_iota(jnp.int32, (HEAD_DIM, PAIR), 1)
    return jnp.where(lane < HEAD_DIM, full[:HEAD_DIM], full[HEAD_DIM:])


def cols(p):
    return slice(p * PAIR, (p + 1) * PAIR)


def kv_kernel(k_ref, v_ref, kv_ref):
    for p in range(kv_ref.shape[0]):
        kv_ref[p] = pack(mm_at(k_ref[:, cols(p)], v_ref[:, cols(p)]))


def scores_kernel(q_ref, k_ref, v_ref, intra_ref):
    rows = q_ref.shape[0]
    masks = halves()
    t = lax.broadcasted_iota(jnp.int32, (rows, rows), 0)
    s = lax.broadcasted_iota(jnp.int32, (rows, rows), 1)
    causal = s <= t
    for p in range(q_ref.shape[1] // PAIR):
        q, k, v = q_ref[:, cols(p)], k_ref[:, cols(p)], v_ref[:, cols(p)]
        sc = mm_bt(stack(q, masks), k)
        sc = jnp.concatenate(
            [jnp.where(causal, sc[:rows], 0.0).astype(BF16), jnp.where(causal, sc[rows:], 0.0).astype(BF16)],
            axis=1,
        )
        intra_ref[:, cols(p)] = mm(sc, stack(v, masks))


def attn_kernel(state_ref, q_ref, intra_ref, gain_ref, g_ref, out_ref, ga_ref, sent_ref, attn_ref, gg_ref):
    rows, width = q_ref.shape
    pairs = width // PAIR
    part = sent_ref.shape[1] - pairs
    masks = halves()
    square = jnp.zeros((rows, PAIR), F32)
    for p in range(pairs):
        low = state_ref[p].astype(BF16)
        attn = intra_ref[:, cols(p)] + mm(q_ref[:, cols(p)], stack(low, masks))
        attn_ref[:, cols(p)] = attn
        square = square + attn * attn
    inv = lax.rsqrt(jnp.sum(square, 1, keepdims=True) * (1.0 / width) + 1e-06)
    dots = jnp.zeros((rows, PAIR), F32)
    for p in range(pairs):
        normed = attn_ref[:, cols(p)] * inv
        attn_ref[:, cols(p)] = normed
        gain = gain_ref[:, cols(p)]
        out_ref[:, cols(p)] = (normed * gain).astype(BF16)
        gn = g_ref[:, cols(p)].astype(F32) * normed
        gg_ref[p : p + 1, :] = jnp.sum(gn, 0, keepdims=True)
        dots = dots + gn * gain
    mean = jnp.sum(dots, 1, keepdims=True) * (1.0 / width)
    for p in range(pairs):
        dn = g_ref[:, cols(p)].astype(F32) * gain_ref[:, cols(p)]
        ga = (inv * (dn - attn_ref[:, cols(p)] * mean)).astype(BF16)
        ga_ref[:, cols(p)] = ga
        per = HEAD_DIM // part
        sent_ref[per * p : per * (p + 1), :part, :] = pack(mm_at(q_ref[:, cols(p)], ga)).reshape(per, part, PAIR)
    own = gg_ref[...]
    for i in range(sent_ref.shape[0]):
        sent_ref[i, part:, :] = own


def local_kernel(state_ref, q_ref, k_ref, v_ref, ga_ref, gq_ref, gk_ref, gv_ref):
    rows = q_ref.shape[0]
    masks = halves()
    t = lax.broadcasted_iota(jnp.int32, (rows, rows), 0)
    s = lax.broadcasted_iota(jnp.int32, (rows, rows), 1)
    causal = s <= t
    causal_t = t <= s

    def both(x, mask):
        return jnp.where(mask, x, 0.0).astype(BF16)

    for p in range(q_ref.shape[1] // PAIR):
        q, k, v, ga = q_ref[:, cols(p)], k_ref[:, cols(p)], v_ref[:, cols(p)], ga_ref[:, cols(p)]
        low = state_ref[p].astype(BF16)
        ga2, q2 = stack(ga, masks), stack(q, masks)
        ds = mm_bt(ga2, v)
        ds = jnp.concatenate([both(ds[:rows], causal), both(ds[rows:], causal)], axis=1)
        gq = mm(ds, stack(k, masks)) + mm_bt(ga, stack(low, masks))
        gq_ref[:, cols(p)] = gq.astype(BF16)
        dst = mm_bt(v, ga2)
        dst = jnp.concatenate([both(dst[:, :rows], causal_t), both(dst[:, rows:], causal_t)], axis=1)
        gk_ref[:, cols(p)] = mm(dst, q2)
        sct = mm_bt(k, q2)
        sct = jnp.concatenate([both(sct[:, :rows], causal_t), both(sct[:, rows:], causal_t)], axis=1)
        gv_ref[:, cols(p)] = mm(sct, ga2)


def later_kernel(later_ref, k_ref, v_ref, gk_ref, gv_ref, gk_out, gv_out):
    masks = halves()
    for p in range(k_ref.shape[1] // PAIR):
        low = stack(later_ref[p].astype(BF16), masks)
        gk_out[:, cols(p)] = (gk_ref[:, cols(p)] + mm_bt(v_ref[:, cols(p)], low)).astype(BF16)
        gv_out[:, cols(p)] = (gv_ref[:, cols(p)] + mm(k_ref[:, cols(p)], low)).astype(BF16)


def prefix_kernel(x_ref, o_ref):
    acc = jnp.zeros(o_ref.shape[1:], F32)
    for i in range(x_ref.shape[0]):
        o_ref[i] = acc
        acc = acc + x_ref[i]


def suffix_kernel(x_ref, o_ref, gg_ref):
    part = o_ref.shape[1]
    total = jnp.zeros(gg_ref.shape, F32)
    acc = jnp.zeros(o_ref.shape[1:], F32)
    for i in reversed(range(x_ref.shape[0])):
        o_ref[i] = acc
        acc = acc + x_ref[i, :part, :]
        total = total + x_ref[i, part:, :]
    gg_ref[...] = total


def call(kernel, outs, args, name, flops, scratch=(), near=None):
    moved = sum(a.size * a.dtype.itemsize for a in args) + sum(o.size * o.dtype.itemsize for o in outs)
    near = (True,) * len(outs) if near is None else near
    shapes = tuple(pltpu.VMEM(o.shape, o.dtype) if n else o for o, n in zip(outs, near))
    single = len(outs) == 1
    return pl.pallas_call(
        kernel,
        out_shape=shapes[0] if single else shapes,
        in_specs=[VMEM] * len(args),
        out_specs=VMEM if single else (VMEM,) * len(outs),
        scratch_shapes=list(scratch),
        compiler_params=pltpu.CompilerParams(vmem_limit_bytes=16 * 1024 * 1024),
        cost_estimate=pl.CostEstimate(flops=flops, bytes_accessed=moved, transcendentals=0),
        name=name,
    )(*(pltpu.with_memory_space_constraint(a, pltpu.VMEM) for a in args))


def exchange(x):
    return lax.all_to_all(x, "ctx", 0, 0, tiled=True)


def make(ctx):
    def per_device(queries, keys, values, gain, grad_out):
        _, rows, width = queries.shape
        pairs = width // PAIR
        q, k, v, g = (x.reshape(rows, width) for x in (queries, keys, values, grad_out))
        gain = gain.reshape(1, width)
        sds = jax.ShapeDtypeStruct
        part = pairs * HEAD_DIM // ctx
        piece = (ctx, part, PAIR)
        state_shape = (pairs, HEAD_DIM, PAIR)
        flops = 2 * rows * rows * width

        kv = call(kv_kernel, (sds(state_shape, F32),), (k, v), "kv", flops)
        sent = exchange(kv.reshape(piece))
        intra = call(scores_kernel, (sds((rows, width), F32),), (q, k, v), "scores", 4 * flops)
        before = call(prefix_kernel, (sds(piece, F32),), (sent,), "prefix", 0)
        state = exchange(before).reshape(state_shape)
        out, ga, sent = call(
            attn_kernel,
            (sds((rows, width), BF16), sds((rows, width), BF16), sds((ctx, part + pairs, PAIR), F32)),
            (state, q, intra, gain, g),
            "attn",
            2 * flops,
            scratch=(pltpu.VMEM((rows, width), F32), pltpu.VMEM((pairs, PAIR), F32)),
            near=(False, True, False),
        )
        sent = exchange(sent)
        gq, gk, gv = call(
            local_kernel,
            (sds((rows, width), BF16), sds((rows, width), F32), sds((rows, width), F32)),
            (state, q, k, v, ga),
            "local",
            10 * flops,
            near=(False, True, True),
        )
        sent, gk, gv = lax.optimization_barrier((sent, gk, gv))
        after, gg = call(suffix_kernel, (sds(piece, F32), sds((pairs, PAIR), F32)), (sent,), "suffix", 0, near=(False, True))
        later = exchange(after).reshape(state_shape)
        gg = lax.psum(gg, "dp")
        later, gg = lax.optimization_barrier((later, gg))
        gk, gv = call(
            later_kernel,
            (sds((rows, width), BF16), sds((rows, width), BF16)),
            (later, k, v, gk, gv),
            "later",
            2 * flops,
            near=(False, False),
        )
        flat = (1, rows, width)
        return out.reshape(flat), gq.reshape(flat), gk.reshape(flat), gv.reshape(flat), gg.reshape(width)

    return per_device


def solution(mesh):
    seq = P("dp", "ctx", None)
    return jax.shard_map(
        make(mesh.shape["ctx"]),
        mesh=mesh,
        in_specs=(seq, seq, seq, P(), seq),
        out_specs=(seq, seq, seq, seq, P()),
        check_vma=False,
    )
```

```python
import functools

import jax
import jax.numpy as jnp
from jax import lax
from jax.experimental import pallas as pl
from jax.experimental.pallas import tpu as pltpu
from jax.sharding import PartitionSpec as P

HEAD_DIM = 64
PAIR = 2 * HEAD_DIM
F32 = jnp.float32
BF16 = jnp.bfloat16
VMEM = pl.BlockSpec(memory_space=pltpu.VMEM)


def mm(a, b):
    return lax.dot_general(a, b, (((1,), (0,)), ((), ())), preferred_element_type=F32)


def mm_bt(a, b):
    return lax.dot_general(a, b, (((1,), (1,)), ((), ())), preferred_element_type=F32)


def mm_at(a, b):
    return lax.dot_general(a, b, (((0,), (0,)), ((), ())), preferred_element_type=F32)


def halves():
    lane = lax.broadcasted_iota(jnp.int32, (1, PAIR), 1)
    first = jnp.where(lane < HEAD_DIM, 1.0, 0.0).astype(BF16)
    second = jnp.where(lane < HEAD_DIM, 0.0, 1.0).astype(BF16)
    return first, second


def stack(x, masks):
    return jnp.concatenate([x * masks[0], x * masks[1]], axis=0)


def pack(full):
    lane = lax.broadcasted_iota(jnp.int32, (HEAD_DIM, PAIR), 1)
    return jnp.where(lane < HEAD_DIM, full[:HEAD_DIM], full[HEAD_DIM:])


def cols(p):
    return slice(p * PAIR, (p + 1) * PAIR)


def kv_kernel(k_hbm, v_hbm, kv_ref, k_ref, v_ref, sems):
    chunks = sems.shape[1]
    wide = k_ref.shape[1] // chunks

    def copies(c):
        at = slice(c * wide, (c + 1) * wide)
        return (
            pltpu.make_async_copy(k_hbm.at[:, at], k_ref.at[:, at], sems.at[0, c]),
            pltpu.make_async_copy(v_hbm.at[:, at], v_ref.at[:, at], sems.at[1, c]),
        )

    for c in range(chunks):
        for copy in copies(c):
            copy.start()
    for c in range(chunks):
        for copy in copies(c):
            copy.wait()
        for p in range(c * wide // PAIR, (c + 1) * wide // PAIR):
            kv_ref[p] = pack(mm_at(k_ref[:, cols(p)], v_ref[:, cols(p)]))


def scores_kernel(q_ref, k_ref, v_ref, gain_ref, intra_ref, gain_out):
    rows = q_ref.shape[0]
    masks = halves()
    t = lax.broadcasted_iota(jnp.int32, (rows, rows), 0)
    s = lax.broadcasted_iota(jnp.int32, (rows, rows), 1)
    causal = s <= t
    for p in range(q_ref.shape[1] // PAIR):
        q, k, v = q_ref[:, cols(p)], k_ref[:, cols(p)], v_ref[:, cols(p)]
        sc = mm_bt(stack(q, masks), k)
        sc = jnp.concatenate(
            [jnp.where(causal, sc[:rows], 0.0).astype(BF16), jnp.where(causal, sc[rows:], 0.0).astype(BF16)],
            axis=1,
        )
        intra_ref[:, cols(p)] = mm(sc, stack(v, masks))
    gain_out[...] = gain_ref[...]


def attn_kernel(state_ref, q_ref, intra_ref, gain_ref, g_ref, out_ref, ga_ref, sent_ref, attn_ref, gg_ref):
    rows, width = q_ref.shape
    pairs = width // PAIR
    part = sent_ref.shape[1] - pairs
    per = HEAD_DIM // part
    masks = halves()
    square = jnp.zeros((rows, PAIR), F32)
    for p in range(pairs):
        low = state_ref[p].astype(BF16)
        attn = intra_ref[:, cols(p)] + mm(q_ref[:, cols(p)], stack(low, masks))
        attn_ref[:, cols(p)] = attn
        square = square + attn * attn
    inv = lax.rsqrt(jnp.sum(square, 1, keepdims=True) * (1.0 / width) + 1e-06)
    dots = jnp.zeros((rows, PAIR), F32)
    for p in range(pairs):
        normed = attn_ref[:, cols(p)] * inv
        attn_ref[:, cols(p)] = normed
        gain = gain_ref[:, cols(p)]
        out_ref[:, cols(p)] = (normed * gain).astype(BF16)
        gn = g_ref[:, cols(p)].astype(F32) * normed
        gg_ref[p : p + 1, :] = jnp.sum(gn, 0, keepdims=True)
        dots = dots + gn * gain
    mean = jnp.sum(dots, 1, keepdims=True) * (1.0 / width)
    for p in range(pairs):
        dn = g_ref[:, cols(p)].astype(F32) * gain_ref[:, cols(p)]
        ga = (inv * (dn - attn_ref[:, cols(p)] * mean)).astype(BF16)
        ga_ref[:, cols(p)] = ga
        sent_ref[per * p : per * (p + 1), :part, :] = pack(mm_at(q_ref[:, cols(p)], ga)).reshape(per, part, PAIR)
    own = gg_ref[...]
    for i in range(sent_ref.shape[0]):
        sent_ref[i, part:, :] = own


def local_kernel(state_ref, q_ref, k_ref, v_ref, ga_ref, gq_ref, gk_ref, gv_ref):
    rows = q_ref.shape[0]
    masks = halves()
    t = lax.broadcasted_iota(jnp.int32, (rows, rows), 0)
    s = lax.broadcasted_iota(jnp.int32, (rows, rows), 1)
    causal = s <= t
    causal_t = t <= s

    def both(x, mask):
        return jnp.where(mask, x, 0.0).astype(BF16)

    for p in range(q_ref.shape[1] // PAIR):
        q, k, v, ga = q_ref[:, cols(p)], k_ref[:, cols(p)], v_ref[:, cols(p)], ga_ref[:, cols(p)]
        low = state_ref[p].astype(BF16)
        ga2, q2 = stack(ga, masks), stack(q, masks)
        ds = mm_bt(ga2, v)
        ds = jnp.concatenate([both(ds[:rows], causal), both(ds[rows:], causal)], axis=1)
        gq = mm(ds, stack(k, masks)) + mm_bt(ga, stack(low, masks))
        gq_ref[:, cols(p)] = gq.astype(BF16)
        dst = mm_bt(v, ga2)
        dst = jnp.concatenate([both(dst[:, :rows], causal_t), both(dst[:, rows:], causal_t)], axis=1)
        gk_ref[:, cols(p)] = mm(dst, q2)
        sct = mm_bt(k, q2)
        sct = jnp.concatenate([both(sct[:, :rows], causal_t), both(sct[:, rows:], causal_t)], axis=1)
        gv_ref[:, cols(p)] = mm(sct, ga2)


def later_kernel(later_ref, k_ref, v_ref, gk_ref, gv_ref, gk_out, gv_out):
    masks = halves()
    for p in range(k_ref.shape[1] // PAIR):
        low = stack(later_ref[p].astype(BF16), masks)
        gk_out[:, cols(p)] = (gk_ref[:, cols(p)] + mm_bt(v_ref[:, cols(p)], low)).astype(BF16)
        gv_out[:, cols(p)] = (gv_ref[:, cols(p)] + mm(k_ref[:, cols(p)], low)).astype(BF16)


def total_kernel(x_ref, o_ref):
    total = x_ref[0]
    for i in range(1, x_ref.shape[0]):
        total = total + x_ref[i]
    o_ref[...] = total


def earlier_kernel(x_ref, *refs):
    outside, o_ref = refs[:-1], refs[-1]
    acc = jnp.zeros(o_ref.shape[1:], F32)
    for ref in outside:
        acc = acc + ref[...]
    for i in range(x_ref.shape[0]):
        o_ref[i] = acc
        acc = acc + x_ref[i]


def later_sums_kernel(x_ref, o_ref, gg_ref):
    part = o_ref.shape[1]
    acc = jnp.zeros((part, PAIR), F32)
    gain = jnp.zeros(gg_ref.shape, F32)
    for i in reversed(range(x_ref.shape[0])):
        o_ref[i] = acc
        acc = acc + x_ref[i, :part, :]
        gain = gain + x_ref[i, part:, :]
    gg_ref[...] = gain


def call(kernel, outs, args, name, flops, scratch=(), near=None, far=False):
    moved = sum(a.size * a.dtype.itemsize for a in args) + sum(o.size * o.dtype.itemsize for o in outs)
    near = (True,) * len(outs) if near is None else near
    shapes = tuple(pltpu.VMEM(o.shape, o.dtype) if n else o for o, n in zip(outs, near))
    single = len(outs) == 1
    space = pltpu.HBM if far else pltpu.VMEM
    return pl.pallas_call(
        kernel,
        out_shape=shapes[0] if single else shapes,
        in_specs=[pl.BlockSpec(memory_space=space)] * len(args),
        out_specs=VMEM if single else (VMEM,) * len(outs),
        scratch_shapes=list(scratch),
        compiler_params=pltpu.CompilerParams(vmem_limit_bytes=16 * 1024 * 1024),
        cost_estimate=pl.CostEstimate(flops=flops, bytes_accessed=moved, transcendentals=0),
        name=name,
    )(*(pltpu.with_memory_space_constraint(a, space) for a in args))


def make(ctx, members):
    groups = ctx // members
    inside = [[g * members + r for r in range(members)] for g in range(groups)]

    def exchange(x, devices=None):
        return lax.all_to_all(x, "ctx", 0, 0, tiled=True, axis_index_groups=devices)

    def from_earlier(total):
        return [
            lax.ppermute(total, "ctx", [(i, i + d * members) for i in range(ctx - d * members)])
            for d in range(1, groups)
        ]

    def per_device(queries, keys, values, gain, grad_out):
        _, rows, width = queries.shape
        pairs = width // PAIR
        q, k, v, g = (x.reshape(rows, width) for x in (queries, keys, values, grad_out))
        gain = gain.reshape(1, width)
        sds = jax.ShapeDtypeStruct
        part = pairs * HEAD_DIM // members
        piece = (members, part, PAIR)
        small = pairs * HEAD_DIM // ctx
        state_shape = (pairs, HEAD_DIM, PAIR)
        flops = 2 * rows * rows * width

        tile = sds((rows, width), BF16)
        kv, k, v = call(
            kv_kernel,
            (sds(state_shape, F32), tile, tile),
            (k, v),
            "kv",
            flops,
            scratch=(pltpu.SemaphoreType.DMA((2, 4)),),
            far=True,
        )
        sent = exchange(kv.reshape(piece), inside)
        total = call(total_kernel, (sds((part, PAIR), F32),), (sent,), "total", 0)
        outside = from_earlier(total)
        intra, gain = call(
            scores_kernel, (sds((rows, width), F32), sds((1, width), F32)), (q, k, v, gain), "scores", 4 * flops
        )
        sent, intra, *outside = lax.optimization_barrier((sent, intra, *outside))
        before = call(earlier_kernel, (sds(piece, F32),), (sent, *outside), "earlier", 0)
        state = exchange(before, inside).reshape(state_shape)
        out, ga, sent = call(
            attn_kernel,
            (sds((rows, width), BF16), sds((rows, width), BF16), sds((ctx, small + pairs, PAIR), F32)),
            (state, q, intra, gain, g),
            "attn",
            2 * flops,
            scratch=(pltpu.VMEM((rows, width), F32), pltpu.VMEM((pairs, PAIR), F32)),
            near=(False, True, False),
        )
        sent = exchange(sent)
        gq, gk, gv = call(
            local_kernel,
            (sds((rows, width), BF16), sds((rows, width), F32), sds((rows, width), F32)),
            (state, q, k, v, ga),
            "local",
            10 * flops,
            near=(False, True, True),
        )
        sent, gk, gv = lax.optimization_barrier((sent, gk, gv))
        after, gg = call(
            later_sums_kernel,
            (sds((ctx, small, PAIR), F32), sds((pairs, PAIR), F32)),
            (sent,),
            "later_sums",
            0,
            near=(False, True),
        )
        later = exchange(after).reshape(state_shape)
        gg = lax.psum(gg, "dp")
        later, gg = lax.optimization_barrier((later, gg))
        gk, gv = call(
            later_kernel,
            (sds((rows, width), BF16), sds((rows, width), BF16)),
            (later, k, v, gk, gv),
            "later",
            2 * flops,
            near=(False, False),
        )
        flat = (1, rows, width)
        return out.reshape(flat), gq.reshape(flat), gk.reshape(flat), gv.reshape(flat), gg.reshape(width)

    return per_device


def solution(mesh):
    seq = P("dp", "ctx", None)
    return jax.shard_map(
        make(mesh.shape["ctx"], 16),
        mesh=mesh,
        in_specs=(seq, seq, seq, P(), seq),
        out_specs=(seq, seq, seq, seq, P()),
        check_vma=False,
    )
```

```python
import functools

import jax
import jax.numpy as jnp
from jax import lax
from jax.experimental import pallas as pl
from jax.experimental.pallas import tpu as pltpu
from jax.sharding import PartitionSpec as P

HEAD_DIM = 64
PAIR = 2 * HEAD_DIM
F32 = jnp.float32
BF16 = jnp.bfloat16
VMEM = pl.BlockSpec(memory_space=pltpu.VMEM)


def mm(a, b):
    return lax.dot_general(a, b, (((1,), (0,)), ((), ())), preferred_element_type=F32)


def mm_bt(a, b):
    return lax.dot_general(a, b, (((1,), (1,)), ((), ())), preferred_element_type=F32)


def mm_at(a, b):
    return lax.dot_general(a, b, (((0,), (0,)), ((), ())), preferred_element_type=F32)


def halves():
    lane = lax.broadcasted_iota(jnp.int32, (1, PAIR), 1)
    first = jnp.where(lane < HEAD_DIM, 1.0, 0.0).astype(BF16)
    second = jnp.where(lane < HEAD_DIM, 0.0, 1.0).astype(BF16)
    return first, second


def stack(x, masks):
    return jnp.concatenate([x * masks[0], x * masks[1]], axis=0)


def pack(full):
    lane = lax.broadcasted_iota(jnp.int32, (HEAD_DIM, PAIR), 1)
    return jnp.where(lane < HEAD_DIM, full[:HEAD_DIM], full[HEAD_DIM:])


def cols(p):
    return slice(p * PAIR, (p + 1) * PAIR)


def kv_kernel(k_hbm, v_hbm, kv_ref, k_ref, v_ref, sems):
    chunks = sems.shape[1]
    wide = k_ref.shape[1] // chunks

    def copies(c):
        at = slice(c * wide, (c + 1) * wide)
        return (
            pltpu.make_async_copy(k_hbm.at[:, at], k_ref.at[:, at], sems.at[0, c]),
            pltpu.make_async_copy(v_hbm.at[:, at], v_ref.at[:, at], sems.at[1, c]),
        )

    for c in range(chunks):
        for copy in copies(c):
            copy.start()
    for c in range(chunks):
        for copy in copies(c):
            copy.wait()
        for p in range(c * wide // PAIR, (c + 1) * wide // PAIR):
            kv_ref[p] = pack(mm_at(k_ref[:, cols(p)], v_ref[:, cols(p)]))


def scores_kernel(q_ref, k_ref, v_ref, gain_ref, intra_ref, gain_out):
    rows = q_ref.shape[0]
    masks = halves()
    t = lax.broadcasted_iota(jnp.int32, (rows, rows), 0)
    s = lax.broadcasted_iota(jnp.int32, (rows, rows), 1)
    causal = s <= t
    for p in range(q_ref.shape[1] // PAIR):
        q, k, v = q_ref[:, cols(p)], k_ref[:, cols(p)], v_ref[:, cols(p)]
        sc = mm_bt(stack(q, masks), k)
        sc = jnp.concatenate(
            [jnp.where(causal, sc[:rows], 0.0).astype(BF16), jnp.where(causal, sc[rows:], 0.0).astype(BF16)],
            axis=1,
        )
        intra_ref[:, cols(p)] = mm(sc, stack(v, masks))
    gain_out[...] = gain_ref[...]


def attn_kernel(state_ref, q_ref, intra_ref, gain_ref, g_ref, out_ref, ga_ref, sums_ref, attn_ref):
    rows, width = q_ref.shape
    pairs = width // PAIR
    masks = halves()
    square = jnp.zeros((rows, PAIR), F32)
    for p in range(pairs):
        low = state_ref[p].astype(BF16)
        attn = intra_ref[:, cols(p)] + mm(q_ref[:, cols(p)], stack(low, masks))
        attn_ref[:, cols(p)] = attn
        square = square + attn * attn
    inv = lax.rsqrt(jnp.sum(square, 1, keepdims=True) * (1.0 / width) + 1e-06)
    dots = jnp.zeros((rows, PAIR), F32)
    for p in range(pairs):
        normed = attn_ref[:, cols(p)] * inv
        attn_ref[:, cols(p)] = normed
        gain = gain_ref[:, cols(p)]
        out_ref[:, cols(p)] = (normed * gain).astype(BF16)
        gn = g_ref[:, cols(p)].astype(F32) * normed
        row = pairs * HEAD_DIM + p
        sums_ref[row : row + 1, :] = jnp.sum(gn, 0, keepdims=True)
        dots = dots + gn * gain
    mean = jnp.sum(dots, 1, keepdims=True) * (1.0 / width)
    for p in range(pairs):
        dn = g_ref[:, cols(p)].astype(F32) * gain_ref[:, cols(p)]
        ga = (inv * (dn - attn_ref[:, cols(p)] * mean)).astype(BF16)
        ga_ref[:, cols(p)] = ga
        sums_ref[p * HEAD_DIM : (p + 1) * HEAD_DIM, :] = pack(mm_at(q_ref[:, cols(p)], ga))


def local_kernel(state_ref, q_ref, k_ref, v_ref, ga_ref, gq_ref, gk_ref, gv_ref):
    rows = q_ref.shape[0]
    masks = halves()
    t = lax.broadcasted_iota(jnp.int32, (rows, rows), 0)
    s = lax.broadcasted_iota(jnp.int32, (rows, rows), 1)
    causal = s <= t
    causal_t = t <= s

    def both(x, mask):
        return jnp.where(mask, x, 0.0).astype(BF16)

    for p in range(q_ref.shape[1] // PAIR):
        q, k, v, ga = q_ref[:, cols(p)], k_ref[:, cols(p)], v_ref[:, cols(p)], ga_ref[:, cols(p)]
        low = state_ref[p].astype(BF16)
        ga2, q2 = stack(ga, masks), stack(q, masks)
        ds = mm_bt(ga2, v)
        ds = jnp.concatenate([both(ds[:rows], causal), both(ds[rows:], causal)], axis=1)
        gq = mm(ds, stack(k, masks)) + mm_bt(ga, stack(low, masks))
        gq_ref[:, cols(p)] = gq.astype(BF16)
        dst = mm_bt(v, ga2)
        dst = jnp.concatenate([both(dst[:, :rows], causal_t), both(dst[:, rows:], causal_t)], axis=1)
        gk_ref[:, cols(p)] = mm(dst, q2)
        sct = mm_bt(k, q2)
        sct = jnp.concatenate([both(sct[:, :rows], causal_t), both(sct[:, rows:], causal_t)], axis=1)
        gv_ref[:, cols(p)] = mm(sct, ga2)


def first_core():
    return lax.rem(lax.axis_index("ctx"), 2) == 0


def merge_kernel(gains, mine_ref, got_ref, o_ref):
    first = first_core()
    chips = o_ref.shape[0]
    part = o_ref.shape[1] - gains
    rows = chips * part
    gain = mine_ref[2 * rows :, :] + got_ref[2 * rows :, :]
    for i in range(chips):
        low, high = slice(i * part, (i + 1) * part), slice(rows + i * part, rows + (i + 1) * part)
        o_ref[i, :part, :] = jnp.where(first, mine_ref[low, :] + got_ref[low, :], mine_ref[high, :] + got_ref[high, :])
        o_ref[i, part:, :] = gain


def later_kernel(sums_ref, got_ref, k_ref, v_ref, gk_ref, gv_ref, gk_out, gv_out):
    first = first_core()
    masks = halves()
    pairs = k_ref.shape[1] // PAIR
    for p in range(pairs):
        core, i = divmod(p, pairs // 2)
        per = sums_ref.shape[0] // (pairs // 2)
        later = sums_ref[per * i : per * (i + 1), core].reshape(HEAD_DIM, PAIR)
        later = later + jnp.where(first, got_ref[p * HEAD_DIM : (p + 1) * HEAD_DIM, :], 0.0)
        low = stack(later.astype(BF16), masks)
        gk_out[:, cols(p)] = (gk_ref[:, cols(p)] + mm_bt(v_ref[:, cols(p)], low)).astype(BF16)
        gv_out[:, cols(p)] = (gv_ref[:, cols(p)] + mm(k_ref[:, cols(p)], low)).astype(BF16)


def total_kernel(x_ref, o_ref):
    total = x_ref[0]
    for i in range(1, x_ref.shape[0]):
        total = total + x_ref[i]
    o_ref[...] = total


def earlier_kernel(x_ref, *refs):
    outside, o_ref = refs[:-1], refs[-1]
    acc = jnp.zeros(o_ref.shape[1:], F32)
    for ref in outside:
        acc = acc + ref[...]
    for i in range(x_ref.shape[0]):
        o_ref[i] = acc
        acc = acc + x_ref[i]


def later_sums_kernel(x_ref, o_ref, gg_ref):
    part = o_ref.shape[1]
    acc = jnp.zeros((part, PAIR), F32)
    gain = jnp.zeros(gg_ref.shape, F32)
    for i in reversed(range(x_ref.shape[0])):
        o_ref[2 * i] = acc
        o_ref[2 * i + 1] = acc
        acc = acc + x_ref[i, :part, :]
        gain = gain + x_ref[i, part:, :]
    gg_ref[...] = gain


def call(kernel, outs, args, name, flops, scratch=(), near=None, far=False):
    moved = sum(a.size * a.dtype.itemsize for a in args) + sum(o.size * o.dtype.itemsize for o in outs)
    near = (True,) * len(outs) if near is None else near
    shapes = tuple(pltpu.VMEM(o.shape, o.dtype) if n else o for o, n in zip(outs, near))
    single = len(outs) == 1
    space = pltpu.HBM if far else pltpu.VMEM
    return pl.pallas_call(
        kernel,
        out_shape=shapes[0] if single else shapes,
        in_specs=[pl.BlockSpec(memory_space=space)] * len(args),
        out_specs=VMEM if single else (VMEM,) * len(outs),
        scratch_shapes=list(scratch),
        compiler_params=pltpu.CompilerParams(vmem_limit_bytes=16 * 1024 * 1024),
        cost_estimate=pl.CostEstimate(flops=flops, bytes_accessed=moved, transcendentals=0),
        name=name,
    )(*(pltpu.with_memory_space_constraint(a, space) for a in args))


def make(ctx, members):
    groups = ctx // members
    chips = ctx // 2
    same_core = [[2 * m + c for m in range(chips)] for c in range(2)]
    neighbour = [(i, i ^ 1) for i in range(ctx)]
    inside = [[g * members + r for r in range(members)] for g in range(groups)]

    def exchange(x, devices=None):
        return lax.all_to_all(x, "ctx", 0, 0, tiled=True, axis_index_groups=devices)

    def from_earlier(total):
        return [
            lax.ppermute(total, "ctx", [(i, i + d * members) for i in range(ctx - d * members)])
            for d in range(1, groups)
        ]

    def per_device(queries, keys, values, gain, grad_out):
        _, rows, width = queries.shape
        pairs = width // PAIR
        q, k, v, g = (x.reshape(rows, width) for x in (queries, keys, values, grad_out))
        gain = gain.reshape(1, width)
        sds = jax.ShapeDtypeStruct
        part = pairs * HEAD_DIM // members
        piece = (members, part, PAIR)
        small = pairs * HEAD_DIM // ctx
        state_shape = (pairs, HEAD_DIM, PAIR)
        flops = 2 * rows * rows * width

        tile = sds((rows, width), BF16)
        kv, k, v = call(
            kv_kernel,
            (sds(state_shape, F32), tile, tile),
            (k, v),
            "kv",
            flops,
            scratch=(pltpu.SemaphoreType.DMA((2, 4)),),
            far=True,
        )
        sent = exchange(kv.reshape(piece), inside)
        total = call(total_kernel, (sds((part, PAIR), F32),), (sent,), "total", 0)
        outside = from_earlier(total)
        intra, gain = call(
            scores_kernel, (sds((rows, width), F32), sds((1, width), F32)), (q, k, v, gain), "scores", 4 * flops
        )
        sent, intra, *outside = lax.optimization_barrier((sent, intra, *outside))
        before = call(earlier_kernel, (sds(piece, F32),), (sent, *outside), "earlier", 0)
        state = exchange(before, inside).reshape(state_shape)
        out, ga, mine = call(
            attn_kernel,
            (tile, tile, sds((pairs * HEAD_DIM + pairs, PAIR), F32)),
            (state, q, intra, gain, g),
            "attn",
            2 * flops,
            scratch=(pltpu.VMEM((rows, width), F32),),
            near=(False, True, True),
        )
        got = lax.ppermute(mine, "ctx", neighbour)
        sent = call(
            functools.partial(merge_kernel, pairs),
            (sds((chips, small + pairs, PAIR), F32),),
            (mine, got),
            "merge",
            0,
            near=(False,),
        )
        sent = exchange(sent, same_core)
        gq, gk, gv = call(
            local_kernel,
            (sds((rows, width), BF16), sds((rows, width), F32), sds((rows, width), F32)),
            (state, q, k, v, ga),
            "local",
            10 * flops,
            near=(False, True, True),
        )
        sent, gk, gv = lax.optimization_barrier((sent, gk, gv))
        after, gg = call(
            later_sums_kernel,
            (sds((ctx, small, PAIR), F32), sds((pairs, PAIR), F32)),
            (sent,),
            "later_sums",
            0,
            near=(False, True),
        )
        later = exchange(after)
        gg = lax.psum(gg, "dp")
        later, gg = lax.optimization_barrier((later, gg))
        gk, gv = call(
            later_kernel,
            (tile, tile),
            (later.reshape(chips, 2, small, PAIR), got, k, v, gk, gv),
            "later",
            2 * flops,
            near=(False, False),
        )
        flat = (1, rows, width)
        return out.reshape(flat), gq.reshape(flat), gk.reshape(flat), gv.reshape(flat), gg.reshape(width)

    return per_device


def solution(mesh):
    seq = P("dp", "ctx", None)
    return jax.shard_map(
        make(mesh.shape["ctx"], 16),
        mesh=mesh,
        in_specs=(seq, seq, seq, P(), seq),
        out_specs=(seq, seq, seq, seq, P()),
        check_vma=False,
    )
```

```python
import functools

import jax
import jax.numpy as jnp
from jax import lax
from jax.experimental import pallas as pl
from jax.experimental.pallas import tpu as pltpu
from jax.sharding import PartitionSpec as P

HEAD_DIM = 64
PAIR = 2 * HEAD_DIM
F32 = jnp.float32
BF16 = jnp.bfloat16
VMEM = pl.BlockSpec(memory_space=pltpu.VMEM)


def mm(a, b):
    return lax.dot_general(a, b, (((1,), (0,)), ((), ())), preferred_element_type=F32)


def mm_bt(a, b):
    return lax.dot_general(a, b, (((1,), (1,)), ((), ())), preferred_element_type=F32)


def mm_at(a, b):
    return lax.dot_general(a, b, (((0,), (0,)), ((), ())), preferred_element_type=F32)


def halves():
    lane = lax.broadcasted_iota(jnp.int32, (1, PAIR), 1)
    first = jnp.where(lane < HEAD_DIM, 1.0, 0.0).astype(BF16)
    second = jnp.where(lane < HEAD_DIM, 0.0, 1.0).astype(BF16)
    return first, second


def stack(x, masks):
    return jnp.concatenate([x * masks[0], x * masks[1]], axis=0)


def pack(full):
    lane = lax.broadcasted_iota(jnp.int32, (HEAD_DIM, PAIR), 1)
    return jnp.where(lane < HEAD_DIM, full[:HEAD_DIM], full[HEAD_DIM:])


def cols(p):
    return slice(p * PAIR, (p + 1) * PAIR)


def kv_kernel(k_hbm, v_hbm, kv_ref, k_ref, v_ref, sems):
    chunks = sems.shape[1]
    wide = k_ref.shape[1] // chunks

    def copies(c):
        at = slice(c * wide, (c + 1) * wide)
        return (
            pltpu.make_async_copy(k_hbm.at[:, at], k_ref.at[:, at], sems.at[0, c]),
            pltpu.make_async_copy(v_hbm.at[:, at], v_ref.at[:, at], sems.at[1, c]),
        )

    for c in range(chunks):
        for copy in copies(c):
            copy.start()
    for c in range(chunks):
        for copy in copies(c):
            copy.wait()
        for p in range(c * wide // PAIR, (c + 1) * wide // PAIR):
            kv_ref[p] = pack(mm_at(k_ref[:, cols(p)], v_ref[:, cols(p)]))


def scores_kernel(q_ref, k_ref, v_ref, gain_ref, intra_ref, gain_out):
    rows = q_ref.shape[0]
    masks = halves()
    t = lax.broadcasted_iota(jnp.int32, (rows, rows), 0)
    s = lax.broadcasted_iota(jnp.int32, (rows, rows), 1)
    causal = s <= t
    for p in range(q_ref.shape[1] // PAIR):
        q, k, v = q_ref[:, cols(p)], k_ref[:, cols(p)], v_ref[:, cols(p)]
        sc = mm_bt(stack(q, masks), k)
        sc = jnp.concatenate(
            [jnp.where(causal, sc[:rows], 0.0).astype(BF16), jnp.where(causal, sc[rows:], 0.0).astype(BF16)],
            axis=1,
        )
        intra_ref[:, cols(p)] = mm(sc, stack(v, masks))
    gain_out[...] = gain_ref[...]


def attn_kernel(state_ref, q_ref, intra_ref, gain_ref, g_ref, attn_ref, ga_ref, sums_ref):
    rows, width = q_ref.shape
    pairs = width // PAIR
    masks = halves()
    square = jnp.zeros((rows, PAIR), F32)
    for p in range(pairs):
        low = state_ref[p].astype(BF16)
        attn = intra_ref[:, cols(p)] + mm(q_ref[:, cols(p)], stack(low, masks))
        attn_ref[:, cols(p)] = attn
        square = square + attn * attn
    inv = lax.rsqrt(jnp.sum(square, 1, keepdims=True) * (1.0 / width) + 1e-06)
    dots = jnp.zeros((rows, PAIR), F32)
    for p in range(pairs):
        normed = attn_ref[:, cols(p)] * inv
        attn_ref[:, cols(p)] = normed
        gain = gain_ref[:, cols(p)]
        gn = g_ref[:, cols(p)].astype(F32) * normed
        row = pairs * HEAD_DIM + p
        sums_ref[row : row + 1, :] = jnp.sum(gn, 0, keepdims=True)
        dots = dots + gn * gain
    mean = jnp.sum(dots, 1, keepdims=True) * (1.0 / width)
    for p in range(pairs):
        dn = g_ref[:, cols(p)].astype(F32) * gain_ref[:, cols(p)]
        ga = (inv * (dn - attn_ref[:, cols(p)] * mean)).astype(BF16)
        ga_ref[:, cols(p)] = ga
        sums_ref[p * HEAD_DIM : (p + 1) * HEAD_DIM, :] = pack(mm_at(q_ref[:, cols(p)], ga))


def local_kernel(state_ref, q_ref, k_ref, v_ref, ga_ref, normed_ref, gain_ref, out_ref, gq_ref, gk_ref, gv_ref):
    rows = q_ref.shape[0]
    masks = halves()
    t = lax.broadcasted_iota(jnp.int32, (rows, rows), 0)
    s = lax.broadcasted_iota(jnp.int32, (rows, rows), 1)
    causal = s <= t
    causal_t = t <= s

    def both(x, mask):
        return jnp.where(mask, x, 0.0).astype(BF16)

    for p in range(q_ref.shape[1] // PAIR):
        q, k, v, ga = q_ref[:, cols(p)], k_ref[:, cols(p)], v_ref[:, cols(p)], ga_ref[:, cols(p)]
        out_ref[:, cols(p)] = (normed_ref[:, cols(p)] * gain_ref[:, cols(p)]).astype(BF16)
        low = state_ref[p].astype(BF16)
        ga2, q2 = stack(ga, masks), stack(q, masks)
        ds = mm_bt(ga2, v)
        ds = jnp.concatenate([both(ds[:rows], causal), both(ds[rows:], causal)], axis=1)
        gq = mm(ds, stack(k, masks)) + mm_bt(ga, stack(low, masks))
        gq_ref[:, cols(p)] = gq.astype(BF16)
        dst = mm_bt(v, ga2)
        dst = jnp.concatenate([both(dst[:, :rows], causal_t), both(dst[:, rows:], causal_t)], axis=1)
        gk_ref[:, cols(p)] = mm(dst, q2)
        sct = mm_bt(k, q2)
        sct = jnp.concatenate([both(sct[:, :rows], causal_t), both(sct[:, rows:], causal_t)], axis=1)
        gv_ref[:, cols(p)] = mm(sct, ga2)


def first_core():
    return lax.rem(lax.axis_index("ctx"), 2) == 0


def merge_kernel(gains, mine_ref, got_ref, o_ref):
    first = first_core()
    chips = o_ref.shape[0]
    part = o_ref.shape[1] - gains
    rows = chips * part
    gain = mine_ref[2 * rows :, :] + got_ref[2 * rows :, :]
    for i in range(chips):
        low, high = slice(i * part, (i + 1) * part), slice(rows + i * part, rows + (i + 1) * part)
        o_ref[i, :part, :] = jnp.where(first, mine_ref[low, :] + got_ref[low, :], mine_ref[high, :] + got_ref[high, :])
        o_ref[i, part:, :] = gain


def later_kernel(sums_ref, got_ref, k_ref, v_ref, gk_ref, gv_ref, gk_out, gv_out):
    first = first_core()
    masks = halves()
    pairs = k_ref.shape[1] // PAIR
    for p in range(pairs):
        core, i = divmod(p, pairs // 2)
        per = sums_ref.shape[0] // (pairs // 2)
        later = sums_ref[per * i : per * (i + 1), core].reshape(HEAD_DIM, PAIR)
        later = later + jnp.where(first, got_ref[p * HEAD_DIM : (p + 1) * HEAD_DIM, :], 0.0)
        low = stack(later.astype(BF16), masks)
        gk_out[:, cols(p)] = (gk_ref[:, cols(p)] + mm_bt(v_ref[:, cols(p)], low)).astype(BF16)
        gv_out[:, cols(p)] = (gv_ref[:, cols(p)] + mm(k_ref[:, cols(p)], low)).astype(BF16)


def total_kernel(x_ref, o_ref):
    total = x_ref[0]
    for i in range(1, x_ref.shape[0]):
        total = total + x_ref[i]
    for i in range(o_ref.shape[0]):
        o_ref[i] = total


def earlier_kernel(x_ref, z_ref, o_ref):
    members = x_ref.shape[0]
    group = lax.div(lax.axis_index("ctx"), members)
    acc = jnp.zeros(o_ref.shape[1:], F32)
    for i in range(z_ref.shape[0] - 1):
        acc = acc + jnp.where(group > i, z_ref[i], 0.0)
    for i in range(members):
        o_ref[i] = acc
        acc = acc + x_ref[i]


def later_sums_kernel(x_ref, o_ref, gg_ref):
    part = o_ref.shape[1]
    acc = jnp.zeros((part, PAIR), F32)
    gain = jnp.zeros(gg_ref.shape, F32)
    for i in reversed(range(x_ref.shape[0])):
        o_ref[2 * i] = acc
        o_ref[2 * i + 1] = acc
        acc = acc + x_ref[i, :part, :]
        gain = gain + x_ref[i, part:, :]
    gg_ref[...] = gain


def call(kernel, outs, args, name, flops, scratch=(), near=None, far=False):
    moved = sum(a.size * a.dtype.itemsize for a in args) + sum(o.size * o.dtype.itemsize for o in outs)
    near = (True,) * len(outs) if near is None else near
    shapes = tuple(pltpu.VMEM(o.shape, o.dtype) if n else o for o, n in zip(outs, near))
    single = len(outs) == 1
    space = pltpu.HBM if far else pltpu.VMEM
    return pl.pallas_call(
        kernel,
        out_shape=shapes[0] if single else shapes,
        in_specs=[pl.BlockSpec(memory_space=space)] * len(args),
        out_specs=VMEM if single else (VMEM,) * len(outs),
        scratch_shapes=list(scratch),
        compiler_params=pltpu.CompilerParams(vmem_limit_bytes=16 * 1024 * 1024),
        cost_estimate=pl.CostEstimate(flops=flops, bytes_accessed=moved, transcendentals=0),
        name=name,
    )(*(pltpu.with_memory_space_constraint(a, space) for a in args))


def make(ctx, members):
    groups = ctx // members
    chips = ctx // 2
    same_core = [[2 * m + c for m in range(chips)] for c in range(2)]
    neighbour = [(i, i ^ 1) for i in range(ctx)]
    across = [[g * members + r for g in range(groups)] for r in range(members)]
    inside = [[g * members + r for r in range(members)] for g in range(groups)]

    def exchange(x, devices=None):
        return lax.all_to_all(x, "ctx", 0, 0, tiled=True, axis_index_groups=devices)

    def per_device(queries, keys, values, gain, grad_out):
        _, rows, width = queries.shape
        pairs = width // PAIR
        q, k, v, g = (x.reshape(rows, width) for x in (queries, keys, values, grad_out))
        gain = gain.reshape(1, width)
        sds = jax.ShapeDtypeStruct
        part = pairs * HEAD_DIM // members
        piece = (members, part, PAIR)
        small = pairs * HEAD_DIM // ctx
        state_shape = (pairs, HEAD_DIM, PAIR)
        flops = 2 * rows * rows * width

        tile = sds((rows, width), BF16)
        kv, k, v = call(
            kv_kernel,
            (sds(state_shape, F32), tile, tile),
            (k, v),
            "kv",
            flops,
            scratch=(pltpu.SemaphoreType.DMA((2, 4)),),
            far=True,
        )
        sent = exchange(kv.reshape(piece), inside)
        totals = call(total_kernel, (sds((groups, part, PAIR), F32),), (sent,), "totals", 0)
        totals = exchange(totals, across)
        intra, gain = call(
            scores_kernel, (sds((rows, width), F32), sds((1, width), F32)), (q, k, v, gain), "scores", 4 * flops
        )
        before = call(earlier_kernel, (sds(piece, F32),), (sent, totals), "earlier", 0)
        state = exchange(before, inside).reshape(state_shape)
        normed, ga, mine = call(
            attn_kernel,
            (sds((rows, width), F32), tile, sds((pairs * HEAD_DIM + pairs, PAIR), F32)),
            (state, q, intra, gain, g),
            "attn",
            2 * flops,
        )
        got = lax.ppermute(mine, "ctx", neighbour)
        sent = call(
            functools.partial(merge_kernel, pairs),
            (sds((chips, small + pairs, PAIR), F32),),
            (mine, got),
            "merge",
            0,
            near=(False,),
        )
        sent = exchange(sent, same_core)
        out, gq, gk, gv = call(
            local_kernel,
            (tile, tile, sds((rows, width), F32), sds((rows, width), F32)),
            (state, q, k, v, ga, normed, gain),
            "local",
            10 * flops,
            near=(False, False, True, True),
        )
        sent, gk, gv = lax.optimization_barrier((sent, gk, gv))
        after, gg = call(
            later_sums_kernel,
            (sds((ctx, small, PAIR), F32), sds((pairs, PAIR), F32)),
            (sent,),
            "later_sums",
            0,
            near=(False, True),
        )
        later = exchange(after)
        gg = lax.psum(gg, "dp")
        later, gg = lax.optimization_barrier((later, gg))
        gk, gv = call(
            later_kernel,
            (tile, tile),
            (later.reshape(chips, 2, small, PAIR), got, k, v, gk, gv),
            "later",
            2 * flops,
            near=(False, False),
        )
        flat = (1, rows, width)
        return out.reshape(flat), gq.reshape(flat), gk.reshape(flat), gv.reshape(flat), gg.reshape(width)

    return per_device


def solution(mesh):
    seq = P("dp", "ctx", None)
    return jax.shard_map(
        make(mesh.shape["ctx"], 16),
        mesh=mesh,
        in_specs=(seq, seq, seq, P(), seq),
        out_specs=(seq, seq, seq, seq, P()),
        check_vma=False,
    )
```

```python
import functools

import jax
import jax.numpy as jnp
from jax import lax
from jax.experimental import pallas as pl
from jax.experimental.pallas import tpu as pltpu
from jax.sharding import PartitionSpec as P

HEAD_DIM = 64
PAIR = 2 * HEAD_DIM
F32 = jnp.float32
BF16 = jnp.bfloat16
VMEM = pl.BlockSpec(memory_space=pltpu.VMEM)


def mm(a, b):
    return lax.dot_general(a, b, (((1,), (0,)), ((), ())), preferred_element_type=F32)


def mm_bt(a, b):
    return lax.dot_general(a, b, (((1,), (1,)), ((), ())), preferred_element_type=F32)


def mm_at(a, b):
    return lax.dot_general(a, b, (((0,), (0,)), ((), ())), preferred_element_type=F32)


def halves():
    lane = lax.broadcasted_iota(jnp.int32, (1, PAIR), 1)
    first = jnp.where(lane < HEAD_DIM, 1.0, 0.0).astype(BF16)
    second = jnp.where(lane < HEAD_DIM, 0.0, 1.0).astype(BF16)
    return first, second


def stack(x, masks):
    return jnp.concatenate([x * masks[0], x * masks[1]], axis=0)


def pack(full):
    lane = lax.broadcasted_iota(jnp.int32, (HEAD_DIM, PAIR), 1)
    return jnp.where(lane < HEAD_DIM, full[:HEAD_DIM], full[HEAD_DIM:])


def cols(p):
    return slice(p * PAIR, (p + 1) * PAIR)


def kv_kernel(k_hbm, v_hbm, gain_hbm, kv_ref, k_ref, v_ref, gain_ref, sems, gain_sem):
    chunks = sems.shape[1]
    wide = k_ref.shape[1] // chunks

    def copies(c):
        at = slice(c * wide, (c + 1) * wide)
        return (
            pltpu.make_async_copy(k_hbm.at[:, at], k_ref.at[:, at], sems.at[0, c]),
            pltpu.make_async_copy(v_hbm.at[:, at], v_ref.at[:, at], sems.at[1, c]),
        )

    for c in range(chunks):
        for copy in copies(c):
            copy.start()
    gain_copy = pltpu.make_async_copy(gain_hbm, gain_ref, gain_sem)
    gain_copy.start()
    for c in range(chunks):
        for copy in copies(c):
            copy.wait()
        for p in range(c * wide // PAIR, (c + 1) * wide // PAIR):
            kv_ref[p] = pack(mm_at(k_ref[:, cols(p)], v_ref[:, cols(p)]))
    gain_copy.wait()


def attn_kernel(state_ref, q_ref, k_ref, v_ref, gain_ref, g_ref, attn_ref, ga_ref, sums_ref):
    rows, width = q_ref.shape
    pairs = width // PAIR
    masks = halves()
    t = lax.broadcasted_iota(jnp.int32, (rows, rows), 0)
    s = lax.broadcasted_iota(jnp.int32, (rows, rows), 1)
    causal = s <= t
    square = jnp.zeros((rows, PAIR), F32)
    for p in range(pairs):
        q, k, v = q_ref[:, cols(p)], k_ref[:, cols(p)], v_ref[:, cols(p)]
        sc = mm_bt(stack(q, masks), k)
        sc = jnp.concatenate(
            [jnp.where(causal, sc[:rows], 0.0).astype(BF16), jnp.where(causal, sc[rows:], 0.0).astype(BF16)],
            axis=1,
        )
        low = state_ref[p].astype(BF16)
        attn = mm(sc, stack(v, masks)) + mm(q, stack(low, masks))
        attn_ref[:, cols(p)] = attn
        square = square + attn * attn
    inv = lax.rsqrt(jnp.sum(square, 1, keepdims=True) * (1.0 / width) + 1e-06)
    dots = jnp.zeros((rows, PAIR), F32)
    for p in range(pairs):
        normed = attn_ref[:, cols(p)] * inv
        attn_ref[:, cols(p)] = normed
        gain = gain_ref[:, cols(p)]
        gn = g_ref[:, cols(p)].astype(F32) * normed
        row = pairs * HEAD_DIM + p
        sums_ref[row : row + 1, :] = jnp.sum(gn, 0, keepdims=True)
        dots = dots + gn * gain
    mean = jnp.sum(dots, 1, keepdims=True) * (1.0 / width)
    for p in range(pairs):
        dn = g_ref[:, cols(p)].astype(F32) * gain_ref[:, cols(p)]
        ga = (inv * (dn - attn_ref[:, cols(p)] * mean)).astype(BF16)
        ga_ref[:, cols(p)] = ga
        sums_ref[p * HEAD_DIM : (p + 1) * HEAD_DIM, :] = pack(mm_at(q_ref[:, cols(p)], ga))


def local_kernel(state_ref, q_ref, k_ref, v_ref, ga_ref, normed_ref, gain_ref, out_ref, gq_ref, gk_ref, gv_ref):
    rows = q_ref.shape[0]
    masks = halves()
    t = lax.broadcasted_iota(jnp.int32, (rows, rows), 0)
    s = lax.broadcasted_iota(jnp.int32, (rows, rows), 1)
    causal = s <= t
    causal_t = t <= s

    def both(x, mask):
        return jnp.where(mask, x, 0.0).astype(BF16)

    for p in range(q_ref.shape[1] // PAIR):
        q, k, v, ga = q_ref[:, cols(p)], k_ref[:, cols(p)], v_ref[:, cols(p)], ga_ref[:, cols(p)]
        out_ref[:, cols(p)] = (normed_ref[:, cols(p)] * gain_ref[:, cols(p)]).astype(BF16)
        low = state_ref[p].astype(BF16)
        ga2, q2 = stack(ga, masks), stack(q, masks)
        ds = mm_bt(ga2, v)
        ds = jnp.concatenate([both(ds[:rows], causal), both(ds[rows:], causal)], axis=1)
        gq = mm(ds, stack(k, masks)) + mm_bt(ga, stack(low, masks))
        gq_ref[:, cols(p)] = gq.astype(BF16)
        dst = mm_bt(v, ga2)
        dst = jnp.concatenate([both(dst[:, :rows], causal_t), both(dst[:, rows:], causal_t)], axis=1)
        gk_ref[:, cols(p)] = mm(dst, q2)
        sct = mm_bt(k, q2)
        sct = jnp.concatenate([both(sct[:, :rows], causal_t), both(sct[:, rows:], causal_t)], axis=1)
        gv_ref[:, cols(p)] = mm(sct, ga2)


def first_core():
    return lax.rem(lax.axis_index("ctx"), 2) == 0


def merge_kernel(gains, mine_ref, got_ref, o_ref):
    first = first_core()
    chips = o_ref.shape[0]
    part = o_ref.shape[1] - gains
    rows = chips * part
    gain = mine_ref[2 * rows :, :] + got_ref[2 * rows :, :]
    for i in range(chips):
        low, high = slice(i * part, (i + 1) * part), slice(rows + i * part, rows + (i + 1) * part)
        o_ref[i, :part, :] = jnp.where(first, mine_ref[low, :] + got_ref[low, :], mine_ref[high, :] + got_ref[high, :])
        o_ref[i, part:, :] = gain


def later_kernel(sums_ref, got_ref, k_ref, v_ref, gk_ref, gv_ref, gk_out, gv_out):
    first = first_core()
    masks = halves()
    pairs = k_ref.shape[1] // PAIR
    for p in range(pairs):
        core, i = divmod(p, pairs // 2)
        per = sums_ref.shape[0] // (pairs // 2)
        later = sums_ref[per * i : per * (i + 1), core].reshape(HEAD_DIM, PAIR)
        later = later + jnp.where(first, got_ref[p * HEAD_DIM : (p + 1) * HEAD_DIM, :], 0.0)
        low = stack(later.astype(BF16), masks)
        gk_out[:, cols(p)] = (gk_ref[:, cols(p)] + mm_bt(v_ref[:, cols(p)], low)).astype(BF16)
        gv_out[:, cols(p)] = (gv_ref[:, cols(p)] + mm(k_ref[:, cols(p)], low)).astype(BF16)


def total_kernel(x_ref, o_ref):
    total = x_ref[0]
    for i in range(1, x_ref.shape[0]):
        total = total + x_ref[i]
    for i in range(o_ref.shape[0]):
        o_ref[i] = total


def earlier_kernel(x_ref, z_ref, o_ref):
    members = x_ref.shape[0]
    group = lax.div(lax.axis_index("ctx"), members)
    acc = jnp.zeros(o_ref.shape[1:], F32)
    for i in range(z_ref.shape[0] - 1):
        acc = acc + jnp.where(group > i, z_ref[i], 0.0)
    for i in range(members):
        o_ref[i] = acc
        acc = acc + x_ref[i]


def later_sums_kernel(x_ref, o_ref, gg_ref):
    part = o_ref.shape[1]
    acc = jnp.zeros((part, PAIR), F32)
    gain = jnp.zeros(gg_ref.shape, F32)
    for i in reversed(range(x_ref.shape[0])):
        o_ref[2 * i] = acc
        o_ref[2 * i + 1] = acc
        acc = acc + x_ref[i, :part, :]
        gain = gain + x_ref[i, part:, :]
    gg_ref[...] = gain


def call(kernel, outs, args, name, flops, scratch=(), near=None, far=False):
    moved = sum(a.size * a.dtype.itemsize for a in args) + sum(o.size * o.dtype.itemsize for o in outs)
    near = (True,) * len(outs) if near is None else near
    shapes = tuple(pltpu.VMEM(o.shape, o.dtype) if n else o for o, n in zip(outs, near))
    single = len(outs) == 1
    space = pltpu.HBM if far else pltpu.VMEM
    return pl.pallas_call(
        kernel,
        out_shape=shapes[0] if single else shapes,
        in_specs=[pl.BlockSpec(memory_space=space)] * len(args),
        out_specs=VMEM if single else (VMEM,) * len(outs),
        scratch_shapes=list(scratch),
        compiler_params=pltpu.CompilerParams(vmem_limit_bytes=16 * 1024 * 1024),
        cost_estimate=pl.CostEstimate(flops=flops, bytes_accessed=moved, transcendentals=0),
        name=name,
    )(*(pltpu.with_memory_space_constraint(a, space) for a in args))


def make(ctx, members):
    groups = ctx // members
    chips = ctx // 2
    same_core = [[2 * m + c for m in range(chips)] for c in range(2)]
    neighbour = [(i, i ^ 1) for i in range(ctx)]
    across = [[g * members + r for g in range(groups)] for r in range(members)]
    inside = [[g * members + r for r in range(members)] for g in range(groups)]

    def exchange(x, devices=None):
        return lax.all_to_all(x, "ctx", 0, 0, tiled=True, axis_index_groups=devices)

    def per_device(queries, keys, values, gain, grad_out):
        _, rows, width = queries.shape
        pairs = width // PAIR
        q, k, v, g = (x.reshape(rows, width) for x in (queries, keys, values, grad_out))
        gain = gain.reshape(1, width)
        sds = jax.ShapeDtypeStruct
        part = pairs * HEAD_DIM // members
        piece = (members, part, PAIR)
        small = pairs * HEAD_DIM // ctx
        state_shape = (pairs, HEAD_DIM, PAIR)
        flops = 2 * rows * rows * width

        tile = sds((rows, width), BF16)
        kv, k, v, gain = call(
            kv_kernel,
            (sds(state_shape, F32), tile, tile, sds((1, width), F32)),
            (k, v, gain),
            "kv",
            flops,
            scratch=(pltpu.SemaphoreType.DMA((2, 4)), pltpu.SemaphoreType.DMA(())),
            far=True,
        )
        sent = exchange(kv.reshape(piece), inside)
        totals = call(total_kernel, (sds((groups, part, PAIR), F32),), (sent,), "totals", 0)
        totals = exchange(totals, across)
        totals = call(total_kernel, (sds((groups, part, PAIR), F32),), (sent,), "totals", 0)
        totals = exchange(totals, across)
        before = call(earlier_kernel, (sds(piece, F32),), (sent, totals), "earlier", 0)
        state = exchange(before, inside).reshape(state_shape)
        normed, ga, mine = call(
            attn_kernel,
            (sds((rows, width), F32), tile, sds((pairs * HEAD_DIM + pairs, PAIR), F32)),
            (state, q, k, v, gain, g),
            "attn",
            6 * flops,
        )
        got = lax.ppermute(mine, "ctx", neighbour)
        out, gq, gk, gv = call(
            local_kernel,
            (tile, tile, sds((rows, width), F32), sds((rows, width), F32)),
            (state, q, k, v, ga, normed, gain),
            "local",
            10 * flops,
            near=(False, False, True, True),
        )
        got, gk, gv = lax.optimization_barrier((got, gk, gv))
        sent = call(
            functools.partial(merge_kernel, pairs),
            (sds((chips, small + pairs, PAIR), F32),),
            (mine, got),
            "merge",
            0,
        )
        sent = exchange(sent, same_core)
        after, gg = call(
            later_sums_kernel,
            (sds((ctx, small, PAIR), F32), sds((pairs, PAIR), F32)),
            (sent,),
            "later_sums",
            0,
            near=(False, True),
        )
        later = exchange(after)
        gg = lax.psum(gg, "dp")
        later, gg = lax.optimization_barrier((later, gg))
        gk, gv = call(
            later_kernel,
            (tile, tile),
            (later.reshape(chips, 2, small, PAIR), got, k, v, gk, gv),
            "later",
            2 * flops,
            near=(False, False),
        )
        flat = (1, rows, width)
        return out.reshape(flat), gq.reshape(flat), gk.reshape(flat), gv.reshape(flat), gg.reshape(width)

    return per_device


def solution(mesh):
    seq = P("dp", "ctx", None)
    return jax.shard_map(
        make(mesh.shape["ctx"], 16),
        mesh=mesh,
        in_specs=(seq, seq, seq, P(), seq),
        out_specs=(seq, seq, seq, seq, P()),
        check_vma=False,
    )
```

```python
import functools

import jax
import jax.numpy as jnp
from jax import lax
from jax.experimental import pallas as pl
from jax.experimental.pallas import tpu as pltpu
from jax.sharding import PartitionSpec as P

HEAD_DIM = 64
PAIR = 2 * HEAD_DIM
F32 = jnp.float32
BF16 = jnp.bfloat16
VMEM = pl.BlockSpec(memory_space=pltpu.VMEM)


def mm(a, b):
    return lax.dot_general(a, b, (((1,), (0,)), ((), ())), preferred_element_type=F32)


def mm_bt(a, b):
    return lax.dot_general(a, b, (((1,), (1,)), ((), ())), preferred_element_type=F32)


def mm_at(a, b):
    return lax.dot_general(a, b, (((0,), (0,)), ((), ())), preferred_element_type=F32)


def halves():
    lane = lax.broadcasted_iota(jnp.int32, (1, PAIR), 1)
    first = jnp.where(lane < HEAD_DIM, 1.0, 0.0).astype(BF16)
    second = jnp.where(lane < HEAD_DIM, 0.0, 1.0).astype(BF16)
    return first, second


def stack(x, masks):
    return jnp.concatenate([x * masks[0], x * masks[1]], axis=0)


def pack(full):
    lane = lax.broadcasted_iota(jnp.int32, (HEAD_DIM, PAIR), 1)
    return jnp.where(lane < HEAD_DIM, full[:HEAD_DIM], full[HEAD_DIM:])


def cols(p):
    return slice(p * PAIR, (p + 1) * PAIR)


def kv_kernel(k_hbm, v_hbm, gain_hbm, kv_ref, k_ref, v_ref, gain_ref, sems, gain_sem):
    chunks = sems.shape[1]
    wide = k_ref.shape[1] // chunks

    def copies(c):
        at = slice(c * wide, (c + 1) * wide)
        return (
            pltpu.make_async_copy(k_hbm.at[:, at], k_ref.at[:, at], sems.at[0, c]),
            pltpu.make_async_copy(v_hbm.at[:, at], v_ref.at[:, at], sems.at[1, c]),
        )

    for c in range(chunks):
        for copy in copies(c):
            copy.start()
    gain_copy = pltpu.make_async_copy(gain_hbm, gain_ref, gain_sem)
    gain_copy.start()
    for c in range(chunks):
        for copy in copies(c):
            copy.wait()
        for p in range(c * wide // PAIR, (c + 1) * wide // PAIR):
            kv_ref[p] = pack(mm_at(k_ref[:, cols(p)], v_ref[:, cols(p)]))
    gain_copy.wait()


def attn_kernel(state_ref, q_ref, k_ref, v_ref, gain_ref, g_ref, attn_ref, ga_ref, sums_ref):
    rows, width = q_ref.shape
    pairs = width // PAIR
    masks = halves()
    t = lax.broadcasted_iota(jnp.int32, (rows, rows), 0)
    s = lax.broadcasted_iota(jnp.int32, (rows, rows), 1)
    causal = s <= t
    square = jnp.zeros((rows, PAIR), F32)
    for p in range(pairs):
        q, k, v = q_ref[:, cols(p)], k_ref[:, cols(p)], v_ref[:, cols(p)]
        sc = mm_bt(stack(q, masks), k)
        sc = jnp.concatenate(
            [jnp.where(causal, sc[:rows], 0.0).astype(BF16), jnp.where(causal, sc[rows:], 0.0).astype(BF16)],
            axis=1,
        )
        low = state_ref[p].astype(BF16)
        attn = mm(sc, stack(v, masks)) + mm(q, stack(low, masks))
        attn_ref[:, cols(p)] = attn
        square = square + attn * attn
    inv = lax.rsqrt(jnp.sum(square, 1, keepdims=True) * (1.0 / width) + 1e-06)
    dots = jnp.zeros((rows, PAIR), F32)
    for p in range(pairs):
        normed = attn_ref[:, cols(p)] * inv
        attn_ref[:, cols(p)] = normed
        gain = gain_ref[:, cols(p)]
        gn = g_ref[:, cols(p)].astype(F32) * normed
        row = pairs * HEAD_DIM + p
        sums_ref[row : row + 1, :] = jnp.sum(gn, 0, keepdims=True)
        dots = dots + gn * gain
    mean = jnp.sum(dots, 1, keepdims=True) * (1.0 / width)
    for p in range(pairs):
        dn = g_ref[:, cols(p)].astype(F32) * gain_ref[:, cols(p)]
        ga = (inv * (dn - attn_ref[:, cols(p)] * mean)).astype(BF16)
        ga_ref[:, cols(p)] = ga
        sums_ref[p * HEAD_DIM : (p + 1) * HEAD_DIM, :] = pack(mm_at(q_ref[:, cols(p)], ga))


def local_kernel(state_ref, q_ref, k_ref, v_ref, ga_ref, normed_ref, gain_ref, out_ref, gq_ref, gk_ref, gv_ref):
    rows = q_ref.shape[0]
    masks = halves()
    t = lax.broadcasted_iota(jnp.int32, (rows, rows), 0)
    s = lax.broadcasted_iota(jnp.int32, (rows, rows), 1)
    causal = s <= t
    causal_t = t <= s

    def both(x, mask):
        return jnp.where(mask, x, 0.0).astype(BF16)

    for p in range(q_ref.shape[1] // PAIR):
        q, k, v, ga = q_ref[:, cols(p)], k_ref[:, cols(p)], v_ref[:, cols(p)], ga_ref[:, cols(p)]
        out_ref[:, cols(p)] = (normed_ref[:, cols(p)] * gain_ref[:, cols(p)]).astype(BF16)
        low = state_ref[p].astype(BF16)
        ga2, q2 = stack(ga, masks), stack(q, masks)
        ds = mm_bt(ga2, v)
        ds = jnp.concatenate([both(ds[:rows], causal), both(ds[rows:], causal)], axis=1)
        gq = mm(ds, stack(k, masks)) + mm_bt(ga, stack(low, masks))
        gq_ref[:, cols(p)] = gq.astype(BF16)
        dst = mm_bt(v, ga2)
        dst = jnp.concatenate([both(dst[:, :rows], causal_t), both(dst[:, rows:], causal_t)], axis=1)
        gk_ref[:, cols(p)] = mm(dst, q2)
        sct = mm_bt(k, q2)
        sct = jnp.concatenate([both(sct[:, :rows], causal_t), both(sct[:, rows:], causal_t)], axis=1)
        gv_ref[:, cols(p)] = mm(sct, ga2)


def first_core():
    return lax.rem(lax.axis_index("ctx"), 2) == 0


def merge_kernel(gains, mine_ref, got_ref, o_ref):
    first = first_core()
    chips = o_ref.shape[0]
    part = o_ref.shape[1] - gains
    rows = chips * part
    gain = mine_ref[2 * rows :, :] + got_ref[2 * rows :, :]
    for i in range(chips):
        low, high = slice(i * part, (i + 1) * part), slice(rows + i * part, rows + (i + 1) * part)
        o_ref[i, :part, :] = jnp.where(first, mine_ref[low, :] + got_ref[low, :], mine_ref[high, :] + got_ref[high, :])
        o_ref[i, part:, :] = gain


def later_kernel(sums_ref, got_ref, k_ref, v_ref, gk_ref, gv_ref, gk_out, gv_out):
    first = first_core()
    masks = halves()
    pairs = k_ref.shape[1] // PAIR
    for p in range(pairs):
        core, i = divmod(p, pairs // 2)
        per = sums_ref.shape[0] // (pairs // 2)
        later = sums_ref[per * i : per * (i + 1), core].reshape(HEAD_DIM, PAIR)
        later = later + jnp.where(first, got_ref[p * HEAD_DIM : (p + 1) * HEAD_DIM, :], 0.0)
        low = stack(later.astype(BF16), masks)
        gk_out[:, cols(p)] = (gk_ref[:, cols(p)] + mm_bt(v_ref[:, cols(p)], low)).astype(BF16)
        gv_out[:, cols(p)] = (gv_ref[:, cols(p)] + mm(k_ref[:, cols(p)], low)).astype(BF16)


def total_kernel(x_ref, o_ref):
    total = x_ref[0]
    for i in range(1, x_ref.shape[0]):
        total = total + x_ref[i]
    for i in range(o_ref.shape[0]):
        o_ref[i] = total


def earlier_kernel(x_ref, z_ref, o_ref):
    members = x_ref.shape[0]
    group = lax.div(lax.axis_index("ctx"), members)
    acc = jnp.zeros(o_ref.shape[1:], F32)
    for i in range(z_ref.shape[0] - 1):
        acc = acc + jnp.where(group > i, z_ref[i], 0.0)
    for i in range(members):
        o_ref[i] = acc
        acc = acc + x_ref[i]


def later_sums_kernel(x_ref, o_ref, gg_ref):
    part = o_ref.shape[1]
    acc = jnp.zeros((part, PAIR), F32)
    gain = jnp.zeros(gg_ref.shape, F32)
    for i in reversed(range(x_ref.shape[0])):
        o_ref[2 * i] = acc
        o_ref[2 * i + 1] = acc
        acc = acc + x_ref[i, :part, :]
        gain = gain + x_ref[i, part:, :]
    gg_ref[...] = gain


def call(kernel, outs, args, name, flops, scratch=(), near=None, far=False):
    moved = sum(a.size * a.dtype.itemsize for a in args) + sum(o.size * o.dtype.itemsize for o in outs)
    near = (True,) * len(outs) if near is None else near
    shapes = tuple(pltpu.VMEM(o.shape, o.dtype) if n else o for o, n in zip(outs, near))
    single = len(outs) == 1
    space = pltpu.HBM if far else pltpu.VMEM
    return pl.pallas_call(
        kernel,
        out_shape=shapes[0] if single else shapes,
        in_specs=[pl.BlockSpec(memory_space=space)] * len(args),
        out_specs=VMEM if single else (VMEM,) * len(outs),
        scratch_shapes=list(scratch),
        compiler_params=pltpu.CompilerParams(vmem_limit_bytes=16 * 1024 * 1024),
        cost_estimate=pl.CostEstimate(flops=flops, bytes_accessed=moved, transcendentals=0),
        name=name,
    )(*(pltpu.with_memory_space_constraint(a, space) for a in args))


def make(ctx, members):
    groups = ctx // members
    chips = ctx // 2
    same_core = [[2 * m + c for m in range(chips)] for c in range(2)]
    neighbour = [(i, i ^ 1) for i in range(ctx)]
    across = [[g * members + r for g in range(groups)] for r in range(members)]
    inside = [[g * members + r for r in range(members)] for g in range(groups)]

    def exchange(x, devices=None):
        return lax.all_to_all(x, "ctx", 0, 0, tiled=True, axis_index_groups=devices)

    def per_device(queries, keys, values, gain, grad_out):
        _, rows, width = queries.shape
        pairs = width // PAIR
        q, k, v, g = (x.reshape(rows, width) for x in (queries, keys, values, grad_out))
        gain = gain.reshape(1, width)
        sds = jax.ShapeDtypeStruct
        part = pairs * HEAD_DIM // members
        piece = (members, part, PAIR)
        small = pairs * HEAD_DIM // ctx
        state_shape = (pairs, HEAD_DIM, PAIR)
        flops = 2 * rows * rows * width

        tile = sds((rows, width), BF16)
        kv, k, v, gain = call(
            kv_kernel,
            (sds(state_shape, F32), tile, tile, sds((1, width), F32)),
            (k, v, gain),
            "kv",
            flops,
            scratch=(pltpu.SemaphoreType.DMA((2, 2)), pltpu.SemaphoreType.DMA(())),
            far=True,
        )
        sent = exchange(kv.reshape(piece), inside)
        totals = call(total_kernel, (sds((groups, part, PAIR), F32),), (sent,), "totals", 0)
        totals = exchange(totals, across)
        totals = call(total_kernel, (sds((groups, part, PAIR), F32),), (sent,), "totals", 0)
        totals = exchange(totals, across)
        before = call(earlier_kernel, (sds(piece, F32),), (sent, totals), "earlier", 0)
        state = exchange(before, inside).reshape(state_shape)
        normed, ga, mine = call(
            attn_kernel,
            (sds((rows, width), F32), tile, sds((pairs * HEAD_DIM + pairs, PAIR), F32)),
            (state, q, k, v, gain, g),
            "attn",
            6 * flops,
        )
        got = lax.ppermute(mine, "ctx", neighbour)
        out, gq, gk, gv = call(
            local_kernel,
            (tile, tile, sds((rows, width), F32), sds((rows, width), F32)),
            (state, q, k, v, ga, normed, gain),
            "local",
            10 * flops,
            near=(False, False, True, True),
        )
        got, gk, gv = lax.optimization_barrier((got, gk, gv))
        sent = call(
            functools.partial(merge_kernel, pairs),
            (sds((chips, small + pairs, PAIR), F32),),
            (mine, got),
            "merge",
            0,
        )
        sent = exchange(sent, same_core)
        after, gg = call(
            later_sums_kernel,
            (sds((ctx, small, PAIR), F32), sds((pairs, PAIR), F32)),
            (sent,),
            "later_sums",
            0,
            near=(False, True),
        )
        later = exchange(after)
        gg = lax.psum(gg, "dp")
        later, gg = lax.optimization_barrier((later, gg))
        gk, gv = call(
            later_kernel,
            (tile, tile),
            (later.reshape(chips, 2, small, PAIR), got, k, v, gk, gv),
            "later",
            2 * flops,
            near=(False, False),
        )
        flat = (1, rows, width)
        return out.reshape(flat), gq.reshape(flat), gk.reshape(flat), gv.reshape(flat), gg.reshape(width)

    return per_device


def solution(mesh):
    seq = P("dp", "ctx", None)
    return jax.shard_map(
        make(mesh.shape["ctx"], 16),
        mesh=mesh,
        in_specs=(seq, seq, seq, P(), seq),
        out_specs=(seq, seq, seq, seq, P()),
        check_vma=False,
    )
```
